512 devices in a mesh: member: 32 (over z, x_lo), tensor: 4 (over x_hi, core), answer: 4 (over y).
Axes of the slice: x: 4 (x_hi: 2, x_lo: 2; x = x_hi * 2 + x_lo), y: 4, z: 16, core: 2. Of those that a mesh axis runs over, the one named last changes fastest.
Arguments:
- master: float32 [5120, 13824], P('member', ('tensor', 'answer')), may hold values from -6 to 6
- left_noise: bfloat16 [4096, 5120], P(('member', 'answer')), may hold values from -5 to 5
- right_noise: bfloat16 [4096, 13824], P(('member', 'answer'), 'tensor'), may hold values from -5 to 5
- returns: float32 [4096, 512], P('member', 'answer'), may hold values from -12 to 12
Outputs:
- new_master: float32 [5120, 13824], P('member', ('tensor', 'answer'))
- rollout: bfloat16 [5120, 13824], P(('member', 'answer'), 'tensor')
The draws below stay inside these ranges and needn't reach their ends.
All inputs are finite; a program needn't handle non-finite values.
Results may differ from the reference program's by a relative error of at most 0.01.
Values may be sent and summed in bfloat16 or wider, within the bound.
No kernel may reach another device: no remote copies, remote signals or barrier semaphores. Data moves between devices by JAX's collectives and lax.ppermute only.
A program may use at most 64 MiB of HBM per device.

```python
import jax
import jax.numpy as jnp
from jax import lax

DMODEL = 5120
DFF = 13824
POP = 4096
ANSWERS = 512


def draw_returns(key, part):
    position = jnp.arange(POP, dtype=jnp.float32) / max(POP - 1, 1)
    rising = 1.0 + 2.0 * position
    base = jax.random.normal(key, (POP, ANSWERS), jnp.float32)
    offset = 0.1
    return jnp.clip((base + offset) * rising[:, None], -12.0, 12.0)


def level_of(rng, shape, cuts, least, high):
    level, own = 1.0, jax.random.fold_in(rng, 6)
    for dim, blocks in cuts:
        draws = jnp.exp(jax.random.uniform(jax.random.fold_in(own, dim), (blocks,), jnp.float32, least / len(cuts), high / len(cuts)))
        level = level * jnp.repeat(draws, shape[dim] // blocks).reshape([-1 if axis == dim else 1 for axis in range(len(shape))])
    return level


def centred(own_key, shape, spread, bound, shards=(), kind=jnp.bfloat16):
    array = spread * jax.random.normal(own_key, shape, jnp.float32)
    if shards:
        array = array * level_of(own_key, shape, shards, -0.22, 0.18)
    return jnp.clip(array, -bound, bound).astype(kind)


def setup_inputs(seed: int = 0) -> dict:
    splits = jax.random.split(jax.random.key(seed), 5)
    return {
        "master": centred(splits[0], (DMODEL, DFF), 1.0, 6.0, ((0, 32), (1, 16)), jnp.float32),
        "left_noise": centred(splits[1], (POP, DMODEL), 1.0, 5.0, ((0, 128),)),
        "right_noise": centred(splits[2], (POP, DFF), 1.0, 5.0, ((0, 128), (1, 4))),
        "returns": draw_returns(jax.random.fold_in(splits[4], 71), 0),
    }


def reference(master, left_noise, right_noise, returns):
    scores = lax.optimization_barrier(jnp.sum(returns, axis=1))
    population = scores.shape[0]
    average = jnp.sum(scores) / population
    variance = jnp.sum(scores * scores) / population - average * average
    fitness = (scores - average) / jnp.sqrt(variance + 1e-05)
    weighted = left_noise.astype(jnp.float32) * fitness[:, None]
    update = lax.dot_general(weighted, right_noise.astype(jnp.float32), (((0,), (0,)), ((), ())), precision=lax.Precision.HIGHEST)
    new_master = master + update / jnp.sqrt(jnp.float32(population))
    return (new_master, new_master.astype(jnp.bfloat16))
```

```python
import jax
import jax.numpy as jnp
from jax import lax
from jax.sharding import Mesh
from jax.sharding import PartitionSpec as P

MEMBER = ("depth", "near")
MEMBER_ANSWER = ("depth", "near", "answer")


def spread(value, axes):
    count = lax.axis_size(axes)
    copies = jnp.broadcast_to(value[None], (count, *value.shape))
    return lax.all_to_all(copies, axes, 0, 0, tiled=True)


def body(master, left_noise, right_noise, returns):
    depth, near, answers = (lax.axis_size(a) for a in ("depth", "near", "answer"))
    share = right_noise.shape[0]
    tile_rows, tile_cols = master.shape
    population = share * depth * near * answers
    near_place = lax.axis_index("near")

    right_part = lax.all_to_all(right_noise, "answer", split_axis=1, concat_axis=0, tiled=True)
    right_cols = lax.all_gather(right_part, "depth", axis=0, tiled=True)

    left_noise, returns, _ = lax.optimization_barrier((left_noise, returns, right_part))
    left_part = lax.all_to_all(left_noise, "depth", split_axis=1, concat_axis=0, tiled=True)
    scores = lax.psum(jnp.sum(returns, axis=1), "answer")
    all_scores = spread(scores, MEMBER)
    average = jnp.sum(all_scores) / population
    variance = jnp.sum(all_scores * all_scores) / population - average * average
    fitness = (all_scores - average) / jnp.sqrt(variance + 1e-05)
    fitness = fitness.reshape(depth, near, answers, share)
    fitness = lax.dynamic_index_in_dim(fitness, near_place, 1, keepdims=False)

    left_rows = spread(left_part, "answer").reshape(answers, depth, share, near * tile_rows)
    weighted = left_rows.transpose(1, 0, 2, 3).astype(jnp.float32) * fitness[..., None]
    weighted = weighted.astype(jnp.bfloat16).reshape(-1, near * tile_rows)
    partial_update = lax.dot_general(
        weighted, right_cols, (((0,), (0,)), ((), ())), preferred_element_type=jnp.float32
    )
    partial_update = partial_update.reshape(near, tile_rows, tile_cols)
    kept = lax.dynamic_index_in_dim(partial_update, near_place, 0, keepdims=False)
    sent = lax.dynamic_index_in_dim(partial_update, 1 - near_place, 0, keepdims=False)
    received = lax.ppermute(sent.astype(jnp.bfloat16), "near", [(0, 1), (1, 0)])
    update = kept + received.astype(jnp.float32)
    new_master = master + update / jnp.sqrt(jnp.float32(population))
    rollout = lax.all_to_all(
        new_master.astype(jnp.bfloat16), "answer", split_axis=0, concat_axis=1, tiled=True
    )
    return (new_master, rollout)


def solution(mesh):
    finer = Mesh(
        mesh.devices.reshape(-1, 2, mesh.shape["tensor"], mesh.shape["answer"]),
        ("depth", "near", "tensor", "answer"),
    )
    placed = (
        P(MEMBER, ("tensor", "answer")),
        P(MEMBER_ANSWER, None),
        P(MEMBER_ANSWER, "tensor"),
        P(MEMBER, "answer"),
    )
    return jax.shard_map(
        body,
        mesh=finer,
        in_specs=placed,
        out_specs=(P(MEMBER, ("tensor", "answer")), P(MEMBER_ANSWER, "tensor")),
        check_vma=False,
    )
```

```python
import math

import jax
import jax.numpy as jnp
from jax import lax
from jax.sharding import Mesh
from jax.sharding import PartitionSpec as P

MEMBER = ("depth", "near")
TENSOR = ("far", "core")
ANSWER = "answer"
RIGHT_SCALE = 2.0**13
PIECE = 2.0**11


def spread(value, axes):
    copies = jnp.broadcast_to(value[None], (lax.axis_size(axes), *value.shape))
    return lax.all_to_all(copies, axes, 0, 0, tiled=True)


def pieces(value):
    high = lax.reduce_precision(value, 5, 10)
    rest = (value - high) * PIECE
    middle = lax.reduce_precision(rest, 5, 10)
    low = (rest - middle) * PIECE
    return jnp.stack([high, middle, low]).astype(jnp.float16)


def joined(parts):
    high, middle, low = (parts[i].astype(jnp.float32) for i in range(3))
    return high + (middle + low / PIECE) / PIECE


def body(master, left_noise, right_noise, returns):
    depth, near, cores, answers = (lax.axis_size(a) for a in ("depth", "near", "core", ANSWER))
    share = right_noise.shape[0]
    tile_rows, tile_cols = master.shape
    block = share * answers
    population = block * depth * near
    near_place = lax.axis_index("near")
    score_scale = 2.0 ** math.floor(math.log2(32768.0 / (12.0 * answers * returns.shape[1])))

    half = left_noise.reshape(share, depth, cores, -1)
    half = lax.dynamic_index_in_dim(half, lax.axis_index("core"), 2, keepdims=False)
    half = lax.all_to_all(half.transpose(1, 0, 2), "depth", 0, 0, tiled=True)
    left_rows = spread(half, ("core", ANSWER)).reshape(cores, answers, depth, share, -1)

    partial_scores = spread(jnp.sum(returns, axis=1), ("near", ANSWER))
    scores = jnp.sum(partial_scores.reshape(near, answers, block), axis=1)

    right_part = lax.all_to_all(right_noise, ANSWER, split_axis=1, concat_axis=0, tiled=True)
    columns = (right_part.astype(jnp.float32).T * RIGHT_SCALE).astype(jnp.float16)
    rows = pieces(scores * score_scale).reshape(3 * near, block)
    filler = jnp.zeros((-(tile_cols + 3 * near) % 16, block), jnp.float16)
    gathered = lax.all_gather(jnp.concatenate([columns, rows, filler]), "depth", axis=0)

    all_scores = gathered[:, tile_cols : tile_cols + 3 * near].reshape(depth, 3, near, block)
    all_scores = joined(jnp.moveaxis(all_scores, 1, 0)) / score_scale
    average = jnp.sum(all_scores) / population
    variance = jnp.sum(all_scores * all_scores) / population - average * average
    fitness = (all_scores - average) / jnp.sqrt(variance + 1e-05)
    fitness = lax.dynamic_index_in_dim(fitness, near_place, 1, keepdims=False)
    fitness = (fitness / RIGHT_SCALE).reshape(depth, answers, share)

    weighted = left_rows.transpose(2, 1, 3, 0, 4).astype(jnp.float32) * fitness[..., None, None]
    weighted = weighted.astype(jnp.bfloat16).reshape(depth, block, near * tile_rows)
    partial_update = lax.dot_general(
        weighted,
        gathered[:, :tile_cols].astype(jnp.bfloat16),
        (((0, 1), (0, 2)), ((), ())),
        preferred_element_type=jnp.float32,
    )
    partial_update = partial_update.reshape(near, tile_rows, tile_cols)
    kept = lax.dynamic_index_in_dim(partial_update, near_place, 0, keepdims=False)
    sent = lax.dynamic_index_in_dim(partial_update, 1 - near_place, 0, keepdims=False)
    received = lax.ppermute(sent.astype(jnp.bfloat16), "near", [(0, 1), (1, 0)])
    update = kept + received.astype(jnp.float32)
    new_master = master + update / jnp.sqrt(jnp.float32(population))
    rollout = lax.all_to_all(
        new_master.astype(jnp.bfloat16), ANSWER, split_axis=0, concat_axis=1, tiled=True
    )
    return (new_master, rollout)


def solution(mesh):
    finer = Mesh(
        mesh.devices.reshape(-1, 2, 2, mesh.shape["tensor"] // 2, mesh.shape["answer"]),
        (*MEMBER, *TENSOR, ANSWER),
    )
    placed = (
        P(MEMBER, (*TENSOR, ANSWER)),
        P((*MEMBER, ANSWER), None),
        P((*MEMBER, ANSWER), TENSOR),
        P(MEMBER, ANSWER),
    )
    return jax.shard_map(
        body,
        mesh=finer,
        in_specs=placed,
        out_specs=(P(MEMBER, (*TENSOR, ANSWER)), P((*MEMBER, ANSWER), TENSOR)),
        check_vma=False,
    )
```

```python
import math

import jax
import jax.numpy as jnp
from jax import lax
from jax.sharding import Mesh
from jax.sharding import PartitionSpec as P

MEMBER = ("depth", "near")
TENSOR = ("far", "core")
ANSWER = "answer"
RIGHT_SCALE = 2.0**13
PIECE = 2.0**11


def spread(value, axes):
    copies = jnp.broadcast_to(value[None], (lax.axis_size(axes), *value.shape))
    return lax.all_to_all(copies, axes, 0, 0, tiled=True)


def pieces(value):
    high = lax.reduce_precision(value, 5, 10)
    rest = (value - high) * PIECE
    middle = lax.reduce_precision(rest, 5, 10)
    low = (rest - middle) * PIECE
    return jnp.stack([high, middle, low]).astype(jnp.float16)


def joined(parts):
    high, middle, low = (parts[i].astype(jnp.float32) for i in range(3))
    return high + (middle + low / PIECE) / PIECE


def body(master, left_noise, right_noise, returns):
    depth, near, cores, answers = (lax.axis_size(a) for a in ("depth", "near", "core", ANSWER))
    share = right_noise.shape[0]
    tile_rows, tile_cols = master.shape
    block = share * answers
    population = block * depth * near
    near_place = lax.axis_index("near")
    score_scale = 2.0 ** math.floor(math.log2(32768.0 / (12.0 * answers * returns.shape[1])))

    half = lax.dynamic_slice_in_dim(
        left_noise, lax.axis_index("core") * (share // cores), share // cores, 0
    )
    half = half.reshape(share // cores, depth, -1).transpose(1, 0, 2)
    half, right_noise, returns = lax.optimization_barrier((half, right_noise, returns))
    half = lax.all_to_all(half, "depth", 0, 0, tiled=True)
    left_rows = spread(half, ("core", ANSWER)).reshape(cores, answers, depth, share // cores, -1)

    answer_place = lax.axis_index(ANSWER)
    outgoing = right_noise.reshape(share, answers, tile_cols).transpose(1, 0, 2)
    incoming = []
    for step in range(answers):
        part = lax.dynamic_index_in_dim(
            outgoing, (answer_place + step) % answers, 0, keepdims=False
        )
        hops = [(i, (i + step) % answers) for i in range(answers)]
        incoming.append(lax.ppermute(part, ANSWER, hops) if step else part)
    incoming = jnp.stack(incoming)
    right_part = jnp.concatenate(
        [
            lax.dynamic_index_in_dim(
                incoming, (answer_place - i) % answers, 0, keepdims=False
            )
            for i in range(answers)
        ]
    )
    scores = jnp.zeros((near, block), jnp.float32)
    scores = lax.dynamic_update_index_in_dim(scores, jnp.sum(returns, axis=1), near_place, 0)
    scores = lax.psum(scores, ("near", ANSWER))

    columns = (right_part.astype(jnp.float32).T * RIGHT_SCALE).astype(jnp.float16)
    rows = pieces(scores * score_scale).reshape(3 * near, block)
    filler = jnp.zeros((-(tile_cols + 3 * near) % 16, block), jnp.float16)
    gathered = lax.all_gather(jnp.concatenate([columns, rows, filler]), "depth", axis=0)

    all_scores = gathered[:, tile_cols : tile_cols + 3 * near].reshape(depth, 3, near, block)
    all_scores = joined(jnp.moveaxis(all_scores, 1, 0)) / score_scale
    average = jnp.sum(all_scores) / population
    variance = jnp.sum(all_scores * all_scores) / population - average * average
    fitness = (all_scores - average) / jnp.sqrt(variance + 1e-05)
    fitness = lax.dynamic_index_in_dim(fitness, near_place, 1, keepdims=False)
    fitness = fitness / (RIGHT_SCALE * math.sqrt(population))

    weighted = gathered[:, :tile_cols].astype(jnp.float32) * fitness[:, None]
    left_rows = left_rows.transpose(2, 1, 0, 3, 4).reshape(depth, block, near * tile_rows)
    partial_update = lax.dot_general(
        left_rows,
        weighted.astype(jnp.bfloat16),
        (((0, 1), (0, 2)), ((), ())),
        preferred_element_type=jnp.float32,
    )
    kept = lax.dynamic_slice_in_dim(partial_update, near_place * tile_rows, tile_rows, 0)
    sent = lax.dynamic_slice_in_dim(partial_update, (1 - near_place) * tile_rows, tile_rows, 0)
    sent = sent.astype(jnp.bfloat16)
    received = lax.ppermute(sent, "near", [(0, 1), (1, 0)])
    kept = master + kept

    parts = kept.astype(jnp.bfloat16)
    parts = jnp.where(near_place == 0, jnp.stack([parts, sent]), jnp.stack([sent, parts]))
    parts = parts.reshape(near * answers, -1, tile_cols)
    parts = lax.all_to_all(parts, ("near", ANSWER), 0, 0, tiled=True)
    parts, received, kept = lax.optimization_barrier((parts, received, kept))
    new_master = kept + received.astype(jnp.float32)
    parts = parts.reshape(near, answers, -1, tile_cols).astype(jnp.float32)
    rollout = (parts[0] + parts[1]).astype(jnp.bfloat16)
    rollout = rollout.transpose(1, 0, 2).reshape(-1, answers * tile_cols)
    return (new_master, rollout)


def solution(mesh):
    finer = Mesh(
        mesh.devices.reshape(-1, 2, 2, mesh.shape["tensor"] // 2, mesh.shape["answer"]),
        (*MEMBER, *TENSOR, ANSWER),
    )
    placed = (
        P(MEMBER, (*TENSOR, ANSWER)),
        P((*MEMBER, ANSWER), None),
        P((*MEMBER, ANSWER), TENSOR),
        P(MEMBER, ANSWER),
    )
    return jax.shard_map(
        body,
        mesh=finer,
        in_specs=placed,
        out_specs=(P(MEMBER, (*TENSOR, ANSWER)), P((*MEMBER, ANSWER), TENSOR)),
        check_vma=False,
    )
```

```python
import math

import jax
import jax.numpy as jnp
from jax import lax
from jax.sharding import Mesh
from jax.sharding import PartitionSpec as P

MEMBER = ("depth", "near")
TENSOR = ("far", "core")
ANSWER = "answer"
RIGHT_SCALE = 2.0**13
PIECE = 2.0**11


def spread(value, axes):
    copies = jnp.broadcast_to(value[None], (lax.axis_size(axes), *value.shape))
    return lax.all_to_all(copies, axes, 0, 0, tiled=True)


def pieces(value, exponent_bits, mantissa_bits, scale):
    high = lax.reduce_precision(value, exponent_bits, mantissa_bits)
    rest = (value - high) * scale
    middle = lax.reduce_precision(rest, exponent_bits, mantissa_bits)
    return jnp.stack([high, middle, (rest - middle) * scale])


def joined(parts):
    high, middle, low = (parts[i].astype(jnp.float32) for i in range(3))
    return high + (middle + low / PIECE) / PIECE


def body(master, left_noise, right_noise, returns):
    depth, near, cores, answers = (lax.axis_size(a) for a in ("depth", "near", "core", ANSWER))
    share = right_noise.shape[0]
    tile_rows, tile_cols = master.shape
    block = share * answers
    population = block * depth * near
    near_place = lax.axis_index("near")
    score_scale = 2.0 ** math.floor(math.log2(32768.0 / (12.0 * answers * returns.shape[1])))

    half = lax.dynamic_slice_in_dim(
        left_noise, lax.axis_index("core") * (share // cores), share // cores, 0
    )
    half = half.reshape(share // cores, depth, -1).transpose(1, 0, 2)
    half, right_noise, returns = lax.optimization_barrier((half, right_noise, returns))
    half = lax.all_to_all(half, "depth", 0, 0, tiled=True)
    left_rows = spread(half, ("core", ANSWER)).reshape(cores, answers, depth, share // cores, -1)

    answer_place = lax.axis_index(ANSWER)
    outgoing = right_noise.reshape(share, answers, tile_cols).transpose(1, 0, 2)
    own_scores = jnp.sum(returns, axis=1)
    near_scores = lax.ppermute(own_scores, "near", [(0, 1), (1, 0)])
    partial_scores = jnp.where(
        near_place == 0,
        jnp.stack([own_scores, near_scores]),
        jnp.stack([near_scores, own_scores]),
    )
    partial_scores = pieces(partial_scores, 8, 7, 1.0).astype(jnp.bfloat16)
    partial_scores = partial_scores.reshape(share, -1)
    incoming = []
    for step in range(answers):
        part = lax.dynamic_index_in_dim(
            outgoing, (answer_place + step) % answers, 0, keepdims=False
        )
        part = jnp.concatenate([part, partial_scores], axis=1)
        hops = [(i, (i + step) % answers) for i in range(answers)]
        incoming.append(lax.ppermute(part, ANSWER, hops) if step else part)
    incoming = jnp.stack(incoming)
    right_part = jnp.concatenate(
        [
            lax.dynamic_index_in_dim(
                incoming[..., :tile_cols], (answer_place - i) % answers, 0, keepdims=False
            )
            for i in range(answers)
        ]
    )
    scores = incoming[..., tile_cols:].astype(jnp.float32)
    scores = jnp.sum(scores.reshape(answers, 3, near, block), axis=(0, 1))

    columns = (right_part.astype(jnp.float32).T * RIGHT_SCALE).astype(jnp.float16)
    rows = pieces(scores * score_scale, 5, 10, PIECE).astype(jnp.float16).reshape(3 * near, block)
    filler = jnp.zeros((-(tile_cols + 3 * near) % 8, block), jnp.float16)
    gathered = lax.all_gather(jnp.concatenate([columns, rows, filler]), "depth", axis=0)

    parts = gathered[:, tile_cols : tile_cols + 3 * near].reshape(depth, 3, near, block)
    all_scores = joined(jnp.moveaxis(parts, 1, 0)) / score_scale
    total, square_total = lax.optimization_barrier(
        tuple(
            jnp.broadcast_to(jnp.sum(value), (1, block))
            for value in (all_scores, all_scores * all_scores)
        )
    )
    average = total / population
    variance = square_total / population - average * average
    fitness = lax.dynamic_index_in_dim(all_scores, near_place, 1, keepdims=False)
    fitness = (fitness - average) / jnp.sqrt(variance + 1e-05)
    fitness = fitness / (RIGHT_SCALE * math.sqrt(population))

    weighted = gathered[:, :tile_cols].astype(jnp.float32) * fitness[:, None]
    left_rows = left_rows.transpose(2, 1, 0, 3, 4).reshape(depth, block, near * tile_rows)
    partial_update = lax.dot_general(
        left_rows,
        weighted.astype(jnp.bfloat16),
        (((0, 1), (0, 2)), ((), ())),
        preferred_element_type=jnp.float32,
    )

    own_rows = lax.broadcasted_iota(jnp.int32, (near, 1, 1), 0) == near_place
    parts = partial_update.reshape(near, tile_rows, tile_cols)
    parts = parts + jnp.where(own_rows, master[None], 0.0)
    sent = lax.dynamic_slice_in_dim(partial_update, (1 - near_place) * tile_rows, tile_rows, 0)
    sent, partial_update = lax.optimization_barrier((sent.astype(jnp.bfloat16), partial_update))
    received = lax.ppermute(sent, "near", [(0, 1), (1, 0)])
    kept = lax.dynamic_slice_in_dim(partial_update, near_place * tile_rows, tile_rows, 0)
    parts, kept = lax.optimization_barrier((parts.astype(jnp.bfloat16), master + kept))
    parts = parts.reshape(near * answers, -1, tile_cols)
    parts = lax.all_to_all(parts, ("near", ANSWER), 0, 0, tiled=True)
    parts, received, kept = lax.optimization_barrier((parts, received, kept))
    new_master = kept + received.astype(jnp.float32)
    parts = parts.reshape(near, answers, -1, tile_cols).astype(jnp.float32)
    rollout = (parts[0] + parts[1]).astype(jnp.bfloat16)
    rollout = rollout.transpose(1, 0, 2).reshape(-1, answers * tile_cols)
    return (new_master, rollout)


def solution(mesh):
    finer = Mesh(
        mesh.devices.reshape(-1, 2, 2, mesh.shape["tensor"] // 2, mesh.shape["answer"]),
        (*MEMBER, *TENSOR, ANSWER),
    )
    placed = (
        P(MEMBER, (*TENSOR, ANSWER)),
        P((*MEMBER, ANSWER), None),
        P((*MEMBER, ANSWER), TENSOR),
        P(MEMBER, ANSWER),
    )
    return jax.shard_map(
        body,
        mesh=finer,
        in_specs=placed,
        out_specs=(P(MEMBER, (*TENSOR, ANSWER)), P((*MEMBER, ANSWER), TENSOR)),
        check_vma=False,
    )
```

```python
import math

import jax
import jax.numpy as jnp
from jax import lax
from jax.sharding import Mesh
from jax.sharding import PartitionSpec as P

MEMBER = ("depth", "near")
TENSOR = ("far", "core")
ANSWER = "answer"
RIGHT_SCALE = 2.0**13
PIECE = 2.0**11


def spread(value, axes):
    copies = jnp.broadcast_to(value[None], (lax.axis_size(axes), *value.shape))
    return lax.all_to_all(copies, axes, 0, 0, tiled=True)


def pieces(value, exponent_bits, mantissa_bits, scale):
    high = lax.reduce_precision(value, exponent_bits, mantissa_bits)
    rest = (value - high) * scale
    middle = lax.reduce_precision(rest, exponent_bits, mantissa_bits)
    return jnp.stack([high, middle, (rest - middle) * scale])


def joined(parts):
    high, middle, low = (parts[i].astype(jnp.float32) for i in range(3))
    return high + (middle + low / PIECE) / PIECE


def body(master, left_noise, right_noise, returns):
    depth, near, cores, answers = (lax.axis_size(a) for a in ("depth", "near", "core", ANSWER))
    share = right_noise.shape[0]
    tile_rows, tile_cols = master.shape
    block = share * answers
    population = block * depth * near
    near_place = lax.axis_index("near")
    score_scale = 2.0 ** math.floor(math.log2(32768.0 / (12.0 * answers * returns.shape[1])))

    half = lax.dynamic_slice_in_dim(
        left_noise, lax.axis_index("core") * (share // cores), share // cores, 0
    )
    half = half.reshape(share // cores, depth, -1).transpose(1, 0, 2)
    own_scores = jnp.sum(returns, axis=1)
    half, right_noise, own_scores = lax.optimization_barrier((half, right_noise, own_scores))
    half = lax.all_to_all(half, "depth", 0, 0, tiled=True)
    left_rows = spread(half, ("core", ANSWER)).reshape(cores, answers, depth, share // cores, -1)

    answer_place = lax.axis_index(ANSWER)
    outgoing = right_noise.reshape(share, answers, tile_cols).transpose(1, 0, 2)
    near_scores = lax.ppermute(own_scores, "near", [(0, 1), (1, 0)])
    partial_scores = jnp.where(
        near_place == 0,
        jnp.stack([own_scores, near_scores]),
        jnp.stack([near_scores, own_scores]),
    )
    partial_scores = pieces(partial_scores, 8, 7, 1.0).astype(jnp.bfloat16)
    partial_scores = partial_scores.reshape(share, -1)
    incoming = []
    for step in range(answers):
        part = lax.dynamic_index_in_dim(
            outgoing, answer_place ^ step, 0, keepdims=False
        )
        part = jnp.concatenate([part, partial_scores], axis=1)
        hops = [(i, i ^ step) for i in range(answers)]
        incoming.append(lax.ppermute(part, ANSWER, hops) if step else part)
    incoming = jnp.stack(incoming)
    right_part = jnp.concatenate(
        [
            lax.dynamic_index_in_dim(
                incoming[..., :tile_cols], answer_place ^ i, 0, keepdims=False
            )
            for i in range(answers)
        ]
    )
    scores = incoming[..., tile_cols:].astype(jnp.float32)
    scores = jnp.sum(scores.reshape(answers, 3, near, block), axis=(0, 1))

    columns = (right_part.astype(jnp.float32).T * RIGHT_SCALE).astype(jnp.float16)
    rows = pieces(scores * score_scale, 5, 10, PIECE).astype(jnp.float16).reshape(3 * near, block)
    filler = jnp.zeros((-(tile_cols + 3 * near) % 8, block), jnp.float16)
    gathered = lax.all_gather(jnp.concatenate([columns, rows, filler]), "depth", axis=0)

    parts = gathered[:, tile_cols : tile_cols + 3 * near].reshape(depth, 3, near, block)
    all_scores = joined(jnp.moveaxis(parts, 1, 0)) / score_scale
    totals = jnp.sum(jnp.stack([all_scores, all_scores * all_scores]), axis=(1, 2, 3))
    totals = lax.optimization_barrier(jnp.broadcast_to(totals[:, None], (2, block)))
    average = totals[:1] / population
    variance = totals[1:] / population - average * average
    fitness = lax.dynamic_index_in_dim(all_scores, near_place, 1, keepdims=False)
    fitness = (fitness - average) / jnp.sqrt(variance + 1e-05)
    fitness = fitness / (RIGHT_SCALE * math.sqrt(population))

    weighted = gathered[:, :tile_cols].astype(jnp.float32) * fitness[:, None]
    left_rows = left_rows.transpose(2, 1, 0, 3, 4).reshape(depth, block, near * tile_rows)
    partial_update = lax.dot_general(
        left_rows,
        weighted.astype(jnp.bfloat16),
        (((0, 1), (0, 2)), ((), ())),
        preferred_element_type=jnp.float32,
    )

    own_rows = lax.broadcasted_iota(jnp.int32, (near, 1, 1), 0) == near_place
    parts = partial_update.reshape(near, tile_rows, tile_cols)
    parts = parts + jnp.where(own_rows, master[None], 0.0)
    sent = lax.dynamic_slice_in_dim(partial_update, (1 - near_place) * tile_rows, tile_rows, 0)
    sent, partial_update = lax.optimization_barrier((sent.astype(jnp.bfloat16), partial_update))
    received = lax.ppermute(sent, "near", [(0, 1), (1, 0)])
    kept = lax.dynamic_slice_in_dim(partial_update, near_place * tile_rows, tile_rows, 0)
    parts, kept = lax.optimization_barrier((parts.astype(jnp.bfloat16), master + kept))
    parts = parts.reshape(near * answers, -1, tile_cols)
    parts = lax.all_to_all(parts, ("near", ANSWER), 0, 0, tiled=True)
    parts, received, kept = lax.optimization_barrier((parts, received, kept))
    new_master = kept + received.astype(jnp.float32)
    parts = parts.reshape(near, answers, -1, tile_cols).astype(jnp.float32)
    rollout = (parts[0] + parts[1]).astype(jnp.bfloat16)
    rollout = rollout.transpose(1, 0, 2).reshape(-1, answers * tile_cols)
    return (new_master, rollout)


def solution(mesh):
    finer = Mesh(
        mesh.devices.reshape(-1, 2, 2, mesh.shape["tensor"] // 2, mesh.shape["answer"]),
        (*MEMBER, *TENSOR, ANSWER),
    )
    placed = (
        P(MEMBER, (*TENSOR, ANSWER)),
        P((*MEMBER, ANSWER), None),
        P((*MEMBER, ANSWER), TENSOR),
        P(MEMBER, ANSWER),
    )
    return jax.shard_map(
        body,
        mesh=finer,
        in_specs=placed,
        out_specs=(P(MEMBER, (*TENSOR, ANSWER)), P((*MEMBER, ANSWER), TENSOR)),
        check_vma=False,
    )
```

```python
import math

import jax
import jax.numpy as jnp
from jax import lax
from jax.sharding import Mesh
from jax.sharding import PartitionSpec as P

MEMBER = ("depth", "near")
TENSOR = ("far", "core")
ANSWER = "answer"
RIGHT_SCALE = 2.0**13
PIECE = 2.0**11


def spread(value, axes):
    copies = jnp.broadcast_to(value[None], (lax.axis_size(axes), *value.shape))
    return lax.all_to_all(copies, axes, 0, 0, tiled=True)


def pieces(value, exponent_bits, mantissa_bits, scale):
    high = lax.reduce_precision(value, exponent_bits, mantissa_bits)
    rest = (value - high) * scale
    middle = lax.reduce_precision(rest, exponent_bits, mantissa_bits)
    return jnp.stack([high, middle, (rest - middle) * scale])


def joined(parts):
    high, middle, low = (parts[i].astype(jnp.float32) for i in range(3))
    return high + (middle + low / PIECE) / PIECE


def body(master, left_noise, right_noise, returns):
    depth, near, cores, answers = (lax.axis_size(a) for a in ("depth", "near", "core", ANSWER))
    share = right_noise.shape[0]
    tile_rows, tile_cols = master.shape
    block = share * answers
    population = block * depth * near
    near_place = lax.axis_index("near")
    score_scale = 2.0 ** math.floor(math.log2(32768.0 / (12.0 * answers * returns.shape[1])))

    half = lax.dynamic_slice_in_dim(
        left_noise, lax.axis_index("core") * (share // cores), share // cores, 0
    )
    half = half.reshape(share // cores, depth, -1).transpose(1, 0, 2)
    own_scores = jnp.sum(returns, axis=1)
    half, right_noise, own_scores = lax.optimization_barrier((half, right_noise, own_scores))
    half = lax.all_to_all(half, "depth", 0, 0, tiled=True)
    left_rows = spread(half, ("core", ANSWER)).reshape(cores, answers, depth, share // cores, -1)

    answer_place = lax.axis_index(ANSWER)
    outgoing = right_noise.reshape(share, answers, tile_cols).transpose(1, 0, 2)
    near_scores = lax.ppermute(own_scores, "near", [(0, 1), (1, 0)])
    partial_scores = jnp.where(
        near_place == 0,
        jnp.stack([own_scores, near_scores]),
        jnp.stack([near_scores, own_scores]),
    )
    partial_scores = pieces(partial_scores, 8, 7, 1.0).astype(jnp.bfloat16)
    partial_scores = partial_scores.reshape(share, -1)
    incoming = []
    for step in range(answers):
        part = lax.dynamic_index_in_dim(
            outgoing, answer_place ^ step, 0, keepdims=False
        )
        part = jnp.concatenate([part, partial_scores], axis=1)
        hops = [(i, i ^ step) for i in range(answers)]
        incoming.append(lax.ppermute(part, ANSWER, hops) if step else part)
    incoming = jnp.stack(incoming)
    right_part = jnp.concatenate(
        [
            lax.dynamic_index_in_dim(
                incoming[..., :tile_cols], answer_place ^ i, 0, keepdims=False
            )
            for i in range(answers)
        ]
    )
    scores = incoming[..., tile_cols:].astype(jnp.float32)
    scores = jnp.sum(scores.reshape(answers, 3, near, block), axis=(0, 1))

    columns = (right_part.astype(jnp.float32).T * RIGHT_SCALE).astype(jnp.float16)
    rows = pieces(scores * score_scale, 5, 10, PIECE).astype(jnp.float16).reshape(3 * near, block)
    filler = jnp.zeros((-(tile_cols + 3 * near) % 8, block), jnp.float16)
    gathered = lax.all_gather(jnp.concatenate([columns, rows, filler]), "depth", axis=0)

    parts = gathered[:, tile_cols : tile_cols + 3 * near].reshape(depth, 3, near, block)
    all_scores = joined(jnp.moveaxis(parts, 1, 0)) / score_scale
    totals = jnp.sum(jnp.stack([all_scores, all_scores * all_scores]), axis=(1, 2, 3))
    totals = lax.optimization_barrier(jnp.broadcast_to(totals[:, None], (2, block)))
    average = totals[:1] / population
    variance = totals[1:] / population - average * average
    fitness = lax.dynamic_index_in_dim(all_scores, near_place, 1, keepdims=False)
    fitness = (fitness - average) / jnp.sqrt(variance + 1e-05)
    fitness = fitness / (RIGHT_SCALE * math.sqrt(population))

    weighted = gathered[:, :tile_cols].astype(jnp.float32) * fitness[:, None]
    left_rows = left_rows.transpose(2, 1, 0, 3, 4).reshape(depth, block, near * tile_rows)
    partial_update = lax.dot_general(
        left_rows,
        weighted.astype(jnp.bfloat16),
        (((0, 1), (0, 2)), ((), ())),
        preferred_element_type=jnp.float32,
    )

    own_rows = lax.broadcasted_iota(jnp.int32, (near, 1, 1), 0) == near_place
    parts = partial_update.reshape(near, tile_rows, tile_cols)
    parts = parts + jnp.where(own_rows, master[None], 0.0)
    sent = lax.dynamic_slice_in_dim(partial_update, (1 - near_place) * tile_rows, tile_rows, 0)
    sent, partial_update = lax.optimization_barrier((sent.astype(jnp.bfloat16), partial_update))
    received = lax.ppermute(sent, "near", [(0, 1), (1, 0)])
    kept = lax.dynamic_slice_in_dim(partial_update, near_place * tile_rows, tile_rows, 0)
    parts, kept = lax.optimization_barrier((parts.astype(jnp.bfloat16), master + kept))
    parts = parts.reshape(near * answers, -1, tile_cols)
    parts = lax.all_to_all(parts, ("near", ANSWER), 0, 0, tiled=True)
    parts = parts.reshape(near, answers, -1, tile_cols).astype(jnp.float32)
    rollout = (parts[0] + parts[1]).astype(jnp.bfloat16)
    rollout = rollout.transpose(1, 0, 2).reshape(-1, answers * tile_cols)
    rollout, received, kept = lax.optimization_barrier((rollout, received, kept))
    new_master = kept + received.astype(jnp.float32)
    return (new_master, rollout)


def solution(mesh):
    finer = Mesh(
        mesh.devices.reshape(-1, 2, 2, mesh.shape["tensor"] // 2, mesh.shape["answer"]),
        (*MEMBER, *TENSOR, ANSWER),
    )
    placed = (
        P(MEMBER, (*TENSOR, ANSWER)),
        P((*MEMBER, ANSWER), None),
        P((*MEMBER, ANSWER), TENSOR),
        P(MEMBER, ANSWER),
    )
    return jax.shard_map(
        body,
        mesh=finer,
        in_specs=placed,
        out_specs=(P(MEMBER, (*TENSOR, ANSWER)), P((*MEMBER, ANSWER), TENSOR)),
        check_vma=False,
    )
```

```python
import math

import jax
import jax.numpy as jnp
from jax import lax
from jax.sharding import Mesh
from jax.sharding import PartitionSpec as P

MEMBER = ("depth", "near")
TENSOR = ("far", "core")
ANSWER = "answer"
RIGHT_SCALE = 2.0**13
PIECE = 2.0**11


def spread(value, axes):
    copies = jnp.broadcast_to(value[None], (lax.axis_size(axes), *value.shape))
    return lax.all_to_all(copies, axes, 0, 0, tiled=True)


def pieces(value, exponent_bits, mantissa_bits, scale):
    high = lax.reduce_precision(value, exponent_bits, mantissa_bits)
    rest = (value - high) * scale
    middle = lax.reduce_precision(rest, exponent_bits, mantissa_bits)
    return jnp.stack([high, middle, (rest - middle) * scale])


def joined(parts):
    high, middle, low = (parts[i].astype(jnp.float32) for i in range(3))
    return high + (middle + low / PIECE) / PIECE


def body(master, left_noise, right_noise, returns):
    depth, near, cores, answers = (lax.axis_size(a) for a in ("depth", "near", "core", ANSWER))
    share = right_noise.shape[0]
    tile_rows, tile_cols = master.shape
    block = share * answers
    population = block * depth * near
    near_place = lax.axis_index("near")
    score_scale = 2.0 ** math.floor(math.log2(32768.0 / (12.0 * answers * returns.shape[1])))

    half = lax.dynamic_slice_in_dim(
        left_noise, lax.axis_index("core") * (share // cores), share // cores, 0
    )
    half = half.reshape(share // cores, depth, -1).transpose(1, 0, 2)
    own_scores = jnp.sum(returns, axis=1)
    half, own_scores = lax.optimization_barrier((half, own_scores))
    half = lax.all_to_all(half, "depth", 0, 0, tiled=True)
    left_rows = spread(half, ("core", ANSWER)).reshape(cores, answers, depth, share // cores, -1)

    answer_place = lax.axis_index(ANSWER)
    outgoing = right_noise.reshape(share, answers, tile_cols).transpose(1, 0, 2)
    near_scores = lax.ppermute(own_scores, "near", [(0, 1), (1, 0)])
    partial_scores = jnp.where(
        near_place == 0,
        jnp.stack([own_scores, near_scores]),
        jnp.stack([near_scores, own_scores]),
    )
    partial_scores = pieces(partial_scores, 8, 7, 1.0).astype(jnp.bfloat16)
    partial_scores = partial_scores.reshape(share, -1)
    incoming = []
    for step in range(answers):
        part = lax.dynamic_index_in_dim(
            outgoing, answer_place ^ step, 0, keepdims=False
        )
        part = jnp.concatenate([part, partial_scores], axis=1)
        hops = [(i, i ^ step) for i in range(answers)]
        incoming.append(lax.ppermute(part, ANSWER, hops) if step else part)
    incoming = jnp.stack(incoming)
    right_part = jnp.concatenate(
        [
            lax.dynamic_index_in_dim(
                incoming[..., :tile_cols], answer_place ^ i, 0, keepdims=False
            )
            for i in range(answers)
        ]
    )
    scores = incoming[..., tile_cols:].astype(jnp.float32)
    scores = jnp.sum(scores.reshape(answers, 3, near, block), axis=(0, 1))

    columns = (right_part.astype(jnp.float32).T * RIGHT_SCALE).astype(jnp.float16)
    rows = pieces(scores * score_scale, 5, 10, PIECE).astype(jnp.float16).reshape(3 * near, block)
    filler = jnp.zeros((-(tile_cols + 3 * near) % 8, block), jnp.float16)
    gathered = lax.all_gather(jnp.concatenate([columns, rows, filler]), "depth", axis=0)

    parts = gathered[:, tile_cols : tile_cols + 3 * near].reshape(depth, 3, near, block)
    all_scores = joined(jnp.moveaxis(parts, 1, 0)) / score_scale
    totals = jnp.sum(jnp.stack([all_scores, all_scores * all_scores]), axis=(1, 2, 3))
    totals = lax.optimization_barrier(jnp.broadcast_to(totals[:, None], (2, block)))
    average = totals[:1] / population
    variance = totals[1:] / population - average * average
    fitness = lax.dynamic_index_in_dim(all_scores, near_place, 1, keepdims=False)
    fitness = (fitness - average) / jnp.sqrt(variance + 1e-05)
    fitness = fitness / (RIGHT_SCALE * math.sqrt(population))

    weighted = gathered[:, :tile_cols].astype(jnp.float32) * fitness[:, None]
    left_rows = left_rows.transpose(2, 1, 0, 3, 4).reshape(depth, block, near * tile_rows)
    partial_update = lax.dot_general(
        left_rows,
        weighted.astype(jnp.bfloat16),
        (((0, 1), (0, 2)), ((), ())),
        preferred_element_type=jnp.float32,
    )

    own_rows = lax.broadcasted_iota(jnp.int32, (near, 1, 1), 0) == near_place
    parts = partial_update.reshape(near, tile_rows, tile_cols)
    parts = parts + jnp.where(own_rows, master[None], 0.0)
    sent = lax.dynamic_slice_in_dim(partial_update, (1 - near_place) * tile_rows, tile_rows, 0)
    sent, partial_update = lax.optimization_barrier((sent.astype(jnp.bfloat16), partial_update))
    received = lax.ppermute(sent, "near", [(0, 1), (1, 0)])
    kept = lax.dynamic_slice_in_dim(partial_update, near_place * tile_rows, tile_rows, 0)
    parts, kept = lax.optimization_barrier((parts.astype(jnp.bfloat16), master + kept))
    parts = parts.reshape(near * answers, -1, tile_cols)
    parts = lax.all_to_all(parts, ("near", ANSWER), 0, 0, tiled=True)
    parts = parts.reshape(near, answers, -1, tile_cols).astype(jnp.float32)
    rollout = (parts[0] + parts[1]).astype(jnp.bfloat16)
    rollout = rollout.transpose(1, 0, 2).reshape(-1, answers * tile_cols)
    rollout, received, kept = lax.optimization_barrier((rollout, received, kept))
    new_master = kept + received.astype(jnp.float32)
    return (new_master, rollout)


def solution(mesh):
    finer = Mesh(
        mesh.devices.reshape(-1, 2, 2, mesh.shape["tensor"] // 2, mesh.shape["answer"]),
        (*MEMBER, *TENSOR, ANSWER),
    )
    placed = (
        P(MEMBER, (*TENSOR, ANSWER)),
        P((*MEMBER, ANSWER), None),
        P((*MEMBER, ANSWER), TENSOR),
        P(MEMBER, ANSWER),
    )
    return jax.shard_map(
        body,
        mesh=finer,
        in_specs=placed,
        out_specs=(P(MEMBER, (*TENSOR, ANSWER)), P((*MEMBER, ANSWER), TENSOR)),
        check_vma=False,
    )
```
